128 devices in a mesh: gx: 8 (over y_lo, x), gy: 16 (over y_hi, z, core).
Axes of the slice: x: 4, y: 4 (y_hi: 2, y_lo: 2; y = y_hi * 2 + y_lo), z: 4, core: 2. Of those that a mesh axis runs over, the one named last changes fastest.
Arguments:
- patches: bfloat16 [1024, 6144], P('gy', 'gx'), may hold values from -2000 to 2000
- norm_gain: float32 [6144], P('gx'), may hold values from 0.5 to 1.5
- w_up: bfloat16 [6144, 24576], P('gx', 'gy'), may hold values from -0.078125 to 0.078125
- bias_up: float32 [24576], P('gy'), may hold values from -4 to 4
- w_down: bfloat16 [24576, 6144], P('gy', 'gx'), may hold values from -0.0390625 to 0.0390625
- bias_down: float32 [6144], P('gx'), may hold values from -4 to 4
- cotangent: bfloat16 [1024, 6144], P('gy', 'gx'), may hold values from -4 to 4
Outputs:
- mlp_out: bfloat16 [1024, 6144], P('gy', 'gx')
- grad_patches: bfloat16 [1024, 6144], P('gy', 'gx')
- grad_gain: float32 [6144], P('gx')
- grad_w_up: float32 [6144, 24576], P('gx', 'gy')
- grad_bias_up: float32 [24576], P('gy')
- grad_w_down: float32 [24576, 6144], P('gy', 'gx')
- grad_bias_down: float32 [6144], P('gx')
The draws below stay inside these ranges and needn't reach their ends.
All inputs are finite; a program needn't handle non-finite values.
Results may differ from the reference program's by a relative error of at most 0.007.
Values may be sent and summed in bfloat16 or wider, within the bound.
A program may use at most 128 MiB of HBM per device.

```python
import jax
import jax.numpy as jnp
from jax import lax

D = 6144
FF = 24576
TOKENS = 1024


def draw_patches(key, part):
    keys = jax.random.split(key, 4)
    rising = jnp.exp(jnp.log(3.0) * jnp.arange(D, dtype=jnp.float32) / D)
    column_scale = rising * jnp.exp(jax.random.uniform(keys[0], (D,), jnp.float32, 0.0, jnp.log(10.0)))
    row_scale = jnp.exp(jax.random.uniform(keys[1], (TOKENS, 1), jnp.float32, 0.0, jnp.log(10.0)))
    noise = jnp.clip(jax.random.normal(keys[2], (TOKENS, D), jnp.float32), -5.0, 5.0)
    offset = jnp.clip(0.3 * jax.random.normal(keys[3], (D,), jnp.float32), -1.0, 1.0)
    return (row_scale * column_scale * (noise + offset)).astype(jnp.bfloat16)


def block_levels(rng, extent, shards, least, largest):
    loudness = 1.0
    for axis_at, shards_of in shards:
        heights = jax.random.uniform(jax.random.fold_in(jax.random.fold_in(rng, 6), axis_at), (shards_of,), jnp.float32, least / len(shards), largest / len(shards))
        loudness = loudness * jnp.repeat(jnp.exp(heights), extent[axis_at] // shards_of).reshape((-1,) + (1,) * (len(extent) - 1 - axis_at))
    return loudness


def centred(stream_key, dims, width, reach, cuts=(), held_as=jnp.bfloat16):
    factor_of = block_levels(stream_key, dims, cuts, -0.22, 0.18) if cuts else 1.0
    values = jax.random.normal(stream_key, dims, jnp.float32) * width * factor_of
    return jnp.minimum(jnp.maximum(values, -reach), reach).astype(held_as)


def setup_inputs(seed: int = 0) -> dict:
    splits = jax.random.split(jax.random.key(seed), 8)
    return {
        "patches": draw_patches(jax.random.fold_in(splits[7], 71), 0),
        "norm_gain": jnp.clip(0.5 + 1.0 * jax.random.uniform(splits[1], (D,), jnp.float32) ** block_levels(splits[1], (D,), ((0, 8),), -0.2, 0.2), 0.5, 1.5),
        "w_up": centred(splits[2], (D, FF), D ** -0.5, 0.078125, ((0, 8), (1, 16))),
        "bias_up": centred(splits[3], (FF,), 1.0, 4.0, ((0, 16),), jnp.float32),
        "w_down": centred(splits[4], (FF, D), FF ** -0.5, 0.0390625, ((0, 16), (1, 8))),
        "bias_down": centred(splits[5], (D,), 1.0, 4.0, ((0, 8),), jnp.float32),
        "cotangent": centred(splits[6], (TOKENS, D), 0.5, 4.0, ((0, 16), (1, 8))),
    }


epsilon = 1e-06
inv_root_two = 0.7071067811865476
inv_root_two_pi = 0.3989422804014327

def gelu_value(hidden):
    return 0.5 * hidden * (1.0 + lax.erf(hidden * inv_root_two))

def gelu_slope(hidden):
    return 0.5 * (1.0 + lax.erf(hidden * inv_root_two)) + hidden * jnp.exp(-0.5 * hidden * hidden) * inv_root_two_pi

def reference(patches, norm_gain, w_up, bias_up, w_down, bias_down, cotangent):
    values = patches.astype(jnp.float32)
    row_mean = lax.optimization_barrier(jnp.sum(values, axis=1, keepdims=True)) / D
    variance = lax.optimization_barrier(jnp.sum(values * values, axis=1, keepdims=True)) / D - row_mean * row_mean
    inv_std = lax.rsqrt(variance + epsilon)
    standard = (values - row_mean) * inv_std
    normed = (standard * norm_gain).astype(jnp.bfloat16)
    hidden = jnp.dot(normed, w_up, preferred_element_type=jnp.float32) + bias_up
    activated = gelu_value(hidden).astype(jnp.bfloat16)
    mlp_out = (jnp.dot(activated, w_down, preferred_element_type=jnp.float32) + bias_down).astype(jnp.bfloat16)
    grad_bias_down = lax.optimization_barrier(jnp.sum(cotangent.astype(jnp.float32), axis=0))
    grad_w_down = jnp.dot(activated.T, cotangent, preferred_element_type=jnp.float32)
    grad_act = jnp.dot(cotangent, w_down.T, preferred_element_type=jnp.float32)
    grad_hidden = (grad_act * gelu_slope(hidden)).astype(jnp.bfloat16)
    grad_bias_up = lax.optimization_barrier(jnp.sum(grad_hidden.astype(jnp.float32), axis=0))
    grad_w_up = jnp.dot(normed.T, grad_hidden, preferred_element_type=jnp.float32)
    grad_normed = jnp.dot(grad_hidden, w_up.T, preferred_element_type=jnp.float32)
    grad_gain = lax.optimization_barrier(jnp.sum(grad_normed * standard, axis=0))
    scaled = grad_normed * norm_gain
    first_mean = lax.optimization_barrier(jnp.sum(scaled, axis=1, keepdims=True)) / D
    second_mean = lax.optimization_barrier(jnp.sum(scaled * standard, axis=1, keepdims=True)) / D
    grad_patches = (inv_std * (scaled - first_mean - standard * second_mean)).astype(jnp.bfloat16)
    return (mlp_out, grad_patches, grad_gain, grad_w_up, grad_bias_up, grad_w_down, grad_bias_down)
```

```python
import functools

import jax
import jax.numpy as jnp
from jax import lax
from jax.experimental import pallas as pl
from jax.experimental.pallas import tpu as pltpu
from jax.sharding import PartitionSpec as P

D = 6144
CHUNKS = 4
MESSAGES = 240

epsilon = 1e-06
inv_root_two = 0.7071067811865476
inv_root_two_pi = 0.3989422804014327

MESH = pl.DeviceIdType.MESH
F32 = jnp.float32
BF16 = jnp.bfloat16


def wide(value):
    return value.astype(F32)


class Mail:
    def __init__(self, send_sems, recv_sems):
        self.send_sems, self.recv_sems, self.sent = send_sems, recv_sems, []

    def send(self, src, dst, device):
        at = len(self.sent)
        copy = pltpu.make_async_remote_copy(
            src_ref=src,
            dst_ref=dst,
            send_sem=self.send_sems.at[at],
            recv_sem=self.recv_sems.at[at],
            device_id=device,
            device_id_type=MESH,
        )
        copy.start()
        self.sent.append(copy)
        return copy

    def finish(self):
        for copy in self.sent:
            copy.wait_send()


def kernel(
    patches, gain, w_up, bias_up, w_down, bias_down, cotangent,
    mlp_out, grad_patches, grad_gain, grad_w_up, grad_bias_up, grad_w_down, grad_bias_down,
    own, standard, wu, wd, cot_all, nor_all,
    ga, ga_y, ga_m1r, ga_m1l, ga_l, ga_r,
    hid, hid_m1r, hid_m1l, hid_l, hid_r, hid_ys, hid_y,
    act, gh,
    mlp_g, mlp_sib, mlp_z, mlp_ys, mlp_y,
    gn_g, gn_sib, gn_z, gn_ys, gn_y, gn,
    stats_a, stats_b, gains, gwu, gwd,
    local_sems, send_sems, recv_sems,
):
    gx, gy = lax.axis_index("gx"), lax.axis_index("gy")
    x, y = lax.rem(gx, 4), lax.div(gx, 4)
    k, z, yh = lax.rem(gy, 2), lax.rem(lax.div(gy, 2), 4), lax.div(gy, 8)
    yo, ko, yho = 1 - y, 1 - k, 1 - yh
    xr, xo, xl = lax.rem(x + 1, 4), lax.rem(x + 2, 4), lax.rem(x + 3, 4)
    right, left, across = (y * 4 + xr, gy), (y * 4 + xl, gy), (yo * 4 + x, gy)
    sibling, far = (gx, yh * 8 + z * 2 + ko), (gx, yho * 8 + z * 2 + k)
    z_at = [lax.rem(z + d, 4) for d in range(4)]
    z_dev = [(gx, yh * 8 + z_at[d] * 2 + k) for d in range(4)]
    mail = Mail(send_sems, recv_sems)

    loads = [pltpu.make_async_copy(patches, own, local_sems.at[0])]
    for c in range(CHUNKS):
        loads.append(
            pltpu.make_async_copy(
                cotangent.at[pl.ds(16 * c, 16)], cot_all.at[c, yh, z, k], local_sems.at[1 + c]
            )
        )
    load_wd = pltpu.make_async_copy(w_down, wd, local_sems.at[5])
    load_wu = pltpu.make_async_copy(w_up, wu, local_sems.at[6])
    for copy in loads + [load_wd, load_wu]:
        copy.start()

    barrier = pltpu.get_barrier_semaphore()
    for d in range(1, 8):
        pl.semaphore_signal(barrier, inc=1, device_id=(lax.rem(gx + d, 8), gy), device_id_type=MESH)
    for d in range(1, 16):
        pl.semaphore_signal(barrier, inc=1, device_id=(gx, lax.rem(gy + d, 16)), device_id_type=MESH)
    pl.semaphore_wait(barrier, 22)

    far_in, z_in, sib_in = {}, {}, {}

    def to_far(name, full, c):
        piece = full.at[c, yh, z, k]
        far_in[name, c] = mail.send(piece, piece, far)

    def to_z(name, full, c):
        far_in[name, c].wait_recv()
        pair = full.at[c, :, z, k]
        z_in[name, c] = [mail.send(pair, pair, z_dev[d]) for d in (1, 2, 3)]

    def to_sibling(name, full, c):
        for copy in z_in[name, c]:
            copy.wait_recv()
        half = full.at[c, :, :, k]
        sib_in[name, c] = mail.send(half, half, sibling)

    def post_stats(box, first, second):
        lane = lax.broadcasted_iota(jnp.int32, (64, 128), 1)
        table = jnp.where(lane == 0, first, jnp.where(lane == 1, second, 0.0))
        table = jnp.concatenate([table, jnp.zeros((64, 128), F32)], axis=0)
        box[gx] = jnp.transpose(table)[:8]
        mine = box.at[gx]
        return [mail.send(mine, mine, (lax.rem(gx + d, 8), gy)) for d in range(1, 8)]

    def read_stats(box, copies):
        for copy in copies:
            copy.wait_recv()
        total = jnp.sum(box[...], axis=0)
        table = jnp.transpose(jnp.concatenate([total, jnp.zeros((120, 128), F32)], axis=0))
        return table[:64, 0:1] / D, table[:64, 1:2] / D

    for c in range(CHUNKS):
        loads[1 + c].wait()
        to_far("cot", cot_all, c)
    loads[0].wait()
    values = wide(own[...])
    stats = post_stats(
        stats_a,
        jnp.sum(values, axis=1, keepdims=True),
        jnp.sum(values * values, axis=1, keepdims=True),
    )

    def columns(total, step, body):
        @pl.loop(0, total // step)
        def _(n):
            body(pl.ds(pl.multiple_of(n * step, step), step))

    def multiply(left_value, right_ref, transposed, out, c, shape, total, step):
        def body(cols):
            if transposed:
                product = lax.dot_general(
                    left_value(), right_ref[cols, :], (((1,), (1,)), ((), ())),
                    preferred_element_type=F32,
                )
            else:
                product = jnp.dot(left_value(), right_ref[:, cols], preferred_element_type=F32)
            out[(c,) + (slice(None),) * (len(shape)) + (cols,)] = product.astype(BF16).reshape(
                shape + (step,)
            )

        columns(total, step, body)

    rows_gx, rows_gy = (4, 2, 32), (2, 4, 2, 16)

    def make_ga(c):
        sib_in["cot", c].wait_recv()
        if c == 0:
            load_wd.wait()
        multiply(lambda: cot_all[c].reshape(256, 768), wd, True, ga, c, rows_gx, 1536, 512)

    def make_hid(c):
        sib_in["nor", c].wait_recv()
        if c == 0:
            load_wu.wait()
        multiply(lambda: nor_all[c].reshape(256, 768), wu, False, hid, c, rows_gx, 1536, 512)

    def make_mlp(c):
        multiply(lambda: act[c].reshape(256, 1536), wd, False, mlp_g, c, rows_gy, 768, 256)

    def make_gn(c):
        multiply(lambda: gh[c].reshape(256, 1536), wu, True, gn_g, c, rows_gy, 768, 256)

    def weight_grad(out, left_ref, right_ref, c, rows, width):
        right_width = 768 + 1536 - rows

        def body(n):
            cols = pl.ds(pl.multiple_of(n * width, width), width)
            left_value = left_ref[(c,) + (slice(None),) * (len(left_ref.shape) - 2) + (cols,)]
            product = lax.dot_general(
                left_value.reshape(256, width), right_ref[c].reshape(256, right_width),
                (((0,), (0,)), ((), ())), preferred_element_type=F32,
            )
            if c == 0:
                out[cols, :] = product
            else:
                out[cols, :] += product

        pl.loop(0, rows // width)(body)

    ga_in, hid_in, act_in, gh_in = {}, {}, {}, {}
    top, low = pl.ds(0, 16), pl.ds(16, 16)

    def ga1(c):
        ga_in[c] = [mail.send(ga.at[c, :, yo], ga_y.at[c], across)]

    def ga2(c):
        ga_in[c][0].wait_recv()
        for t in (xo, xr, xl):
            ga[c, t, y] = (wide(ga[c, t, y]) + wide(ga_y[c, t])).astype(BF16)
        ga_in[c] = [
            mail.send(ga.at[c, xo, y, top], ga_m1r.at[c], right),
            mail.send(ga.at[c, xo, y, low], ga_m1l.at[c], left),
            mail.send(ga.at[c, xr, y, low], ga_l.at[c, low], right),
            mail.send(ga.at[c, xl, y, top], ga_r.at[c, top], left),
        ]

    def ga3(c):
        ga_in[c][0].wait_recv()
        ga[c, xr, y, top] = (wide(ga[c, xr, y, top]) + wide(ga_m1r[c])).astype(BF16)
        first = mail.send(ga.at[c, xr, y, top], ga_l.at[c, top], right)
        ga_in[c][1].wait_recv()
        ga[c, xl, y, low] = (wide(ga[c, xl, y, low]) + wide(ga_m1l[c])).astype(BF16)
        second = mail.send(ga.at[c, xl, y, low], ga_r.at[c, low], left)
        ga_in[c] = ga_in[c][2:] + [first, second]

    def ga4(c):
        for copy in ga_in[c]:
            copy.wait_recv()

    def hid1(c):
        hid_in[c] = [
            mail.send(hid.at[c, xo, 0], hid_m1r.at[c], right),
            mail.send(hid.at[c, xo, 1], hid_m1l.at[c], left),
            mail.send(hid.at[c, xr, 1], hid_l.at[c, 1], right),
            mail.send(hid.at[c, xl, 0], hid_r.at[c, 0], left),
        ]

    def hid2(c):
        hid_in[c][0].wait_recv()
        hid[c, xr, 0] = (wide(hid[c, xr, 0]) + wide(hid_m1r[c])).astype(BF16)
        first = mail.send(hid.at[c, xr, 0], hid_l.at[c, 0], right)
        hid_in[c][1].wait_recv()
        hid[c, xl, 1] = (wide(hid[c, xl, 1]) + wide(hid_m1l[c])).astype(BF16)
        second = mail.send(hid.at[c, xl, 1], hid_r.at[c, 1], left)
        hid_in[c] = hid_in[c][2:] + [first, second]

    def hid_sum(c, at):
        return wide(hid[c, x, at]) + wide(hid_l[c, at]) + wide(hid_r[c, at])

    def hid3(c):
        for copy in hid_in[c]:
            copy.wait_recv()
        hid_ys[c] = hid_sum(c, yo).astype(BF16)
        hid_in[c] = [mail.send(hid_ys.at[c], hid_y.at[c], across)]

    def hid4(c):
        hid_in[c][0].wait_recv()

    def activate(c):
        ga4(c)
        hid4(c)
        hidden = hid_sum(c, y) + wide(hid_y[c]) + bias_up[...]
        phi = 0.5 * (1.0 + lax.erf(hidden * inv_root_two))
        act[c, x, y] = (hidden * phi).astype(BF16)
        total = wide(ga[c, x, y]) + wide(ga_y[c, x]) + wide(ga_l[c]) + wide(ga_r[c])
        slope = phi + hidden * jnp.exp(-0.5 * hidden * hidden) * inv_root_two_pi
        gh[c, x, y] = (total * slope).astype(BF16)

    def act1(c):
        piece = act.at[c, x, y]
        act_in[c] = [mail.send(piece, piece, device) for device in (across, right, left)]

    def act2(c):
        act_in[c][0].wait_recv()
        piece = act.at[c, x, yo]
        act_in[c] = act_in[c][1:] + [mail.send(piece, piece, device) for device in (right, left)]

    def act3(c):
        for copy in act_in[c]:
            copy.wait_recv()
        act_in[c] = [
            mail.send(act.at[c, xl, 0], act.at[c, xl, 0], right),
            mail.send(act.at[c, xr, 1], act.at[c, xr, 1], left),
        ]

    def act4(c):
        for copy in act_in[c]:
            copy.wait_recv()

    def gh1(c):
        piece = gh.at[c, x, y]
        gh_in[c] = [mail.send(piece, piece, device) for device in (right, left, across)]

    def gh2(c):
        from_left, from_right, from_across = gh_in[c]
        from_left.wait_recv()
        first = mail.send(gh.at[c, xl, y, top], gh.at[c, xl, y, top], right)
        across_left = mail.send(gh.at[c, xl, y], gh.at[c, xl, y], across)
        from_right.wait_recv()
        second = mail.send(gh.at[c, xr, y, low], gh.at[c, xr, y, low], left)
        across_right = mail.send(gh.at[c, xr, y], gh.at[c, xr, y], across)
        gh_in[c] = [first, second, from_across, across_left, across_right]

    def gh3(c):
        gh_in[c][0].wait_recv()
        gh_in[c][1].wait_recv()
        gh_in[c] = gh_in[c][2:] + [mail.send(gh.at[c, xo, y], gh.at[c, xo, y], across)]

    def gh4(c):
        for copy in gh_in[c]:
            copy.wait_recv()

    boxes = {"mlp": (mlp_g, mlp_sib, mlp_z, mlp_ys, mlp_y), "gn": (gn_g, gn_sib, gn_z, gn_ys, gn_y)}
    back = {}

    def back0(name, c):
        part, sib, _, _, _ = boxes[name]
        back[name, c] = mail.send(part.at[c, :, :, ko], sib.at[c], sibling)

    def back1(name, c):
        part, sib, z_box, _, _ = boxes[name]
        back[name, c].wait_recv()
        part[c, :, :, k] = (wide(part[c, :, :, k]) + wide(sib[c])).astype(BF16)
        back[name, c] = [
            mail.send(part.at[c, :, z_at[d], k], z_box.at[c, z], z_dev[d]) for d in (1, 2, 3)
        ]

    def back_sum(name, c, at):
        part, _, z_box, _, _ = boxes[name]
        total = wide(part[c, at, z, k])
        for d in (1, 2, 3):
            total = total + wide(z_box[c, z_at[d], at])
        return total

    def back2(name, c):
        _, _, _, ys, y_box = boxes[name]
        for copy in back[name, c]:
            copy.wait_recv()
        ys[c] = back_sum(name, c, yho).astype(BF16)
        back[name, c] = mail.send(ys.at[c], y_box.at[c], far)

    def back3(name, c):
        back[name, c].wait_recv()
        total = back_sum(name, c, yh) + wide(boxes[name][4][c])
        if name == "mlp":
            mlp_out[pl.ds(16 * c, 16), :] = (total + bias_down[...]).astype(BF16)
        else:
            gn[pl.ds(16 * c, 16), :] = total

    for c in range(CHUNKS):
        to_z("cot", cot_all, c)
    row_mean, square_mean = read_stats(stats_a, stats)
    inv_std = lax.rsqrt(square_mean - row_mean * row_mean + epsilon)
    normal = (values - row_mean) * inv_std
    standard[...] = normal
    normed = (normal * gain[...]).astype(BF16)
    for c in range(CHUNKS):
        nor_all[c, yh, z, k] = normed[16 * c : 16 * c + 16]
        to_far("nor", nor_all, c)

    def cot3(c):
        to_sibling("cot", cot_all, c)

    def nor3(c):
        to_sibling("nor", nor_all, c)

    def start_ga(c):
        make_ga(c)
        ga1(c)

    def start_hid(c):
        make_hid(c)
        hid1(c)

    def start_act(c):
        activate(c)
        act1(c)
        gh1(c)

    def start_mlp(c):
        act4(c)
        make_mlp(c)
        back0("mlp", c)

    def start_gn(c):
        gh4(c)
        make_gn(c)
        back0("gn", c)

    def grad_down(c):
        weight_grad(gwd, act, cot_all, c, 1536, 256)

    def grad_up(c):
        weight_grad(gwu, nor_all, gh, c, 768, 256)

    cot3(0)
    start_ga(0)
    cot3(1)
    for c in range(CHUNKS):
        to_z("nor", nor_all, c)
    start_ga(1)
    cot3(2)
    nor3(0)
    ga2(0)
    start_hid(0)
    start_ga(2)
    cot3(3)
    nor3(1)
    ga3(0)
    ga2(1)
    hid2(0)
    start_hid(1)
    start_ga(3)
    nor3(2)
    ga3(1)
    ga2(2)
    hid3(0)
    hid2(1)
    start_hid(2)
    start_act(0)
    nor3(3)
    ga3(2)
    ga2(3)
    hid3(1)
    hid2(2)
    act2(0)
    start_hid(3)
    start_act(1)
    gh2(0)
    ga3(3)
    hid3(2)
    hid2(3)
    act3(0)
    act2(1)
    start_act(2)
    gh3(0)
    gh2(1)
    hid3(3)
    start_mlp(0)
    act3(1)
    act2(2)
    start_act(3)
    start_gn(0)
    grad_down(0)
    gh3(1)
    gh2(2)
    back1("mlp", 0)
    start_mlp(1)
    act3(2)
    act2(3)
    back1("gn", 0)
    grad_up(0)
    start_gn(1)
    gh3(2)
    gh2(3)
    back2("mlp", 0)
    back1("mlp", 1)
    grad_down(1)
    start_mlp(2)
    act3(3)
    back2("gn", 0)
    back1("gn", 1)
    start_gn(2)
    gh3(3)
    grad_up(1)
    back3("mlp", 0)
    back2("mlp", 1)
    back1("mlp", 2)
    start_mlp(3)
    grad_down(2)
    back3("gn", 0)
    back2("gn", 1)
    back1("gn", 2)
    grad_up(2)
    back3("mlp", 1)
    back2("mlp", 2)
    start_gn(3)
    back1("mlp", 3)
    grad_down(3)
    store_wd = pltpu.make_async_copy(gwd, grad_w_down, local_sems.at[7])
    store_wd.start()
    back3("gn", 1)
    back2("gn", 2)
    back1("gn", 3)
    back3("mlp", 2)
    back2("mlp", 3)
    back3("gn", 2)
    grad_up(3)
    store_wu = pltpu.make_async_copy(gwu, grad_w_up, local_sems.at[8])
    store_wu.start()
    back2("gn", 3)
    back3("mlp", 3)
    back3("gn", 3)

    grad_normed = gn[...]
    normal = standard[...]
    weighted = grad_normed * normal
    gains[gy] = jnp.sum(weighted.reshape(8, 8, 768), axis=0)
    scaled = grad_normed * gain[...]
    stats = post_stats(
        stats_b,
        jnp.sum(scaled, axis=1, keepdims=True),
        jnp.sum(scaled * normal, axis=1, keepdims=True),
    )
    mine = gains.at[gy]
    gain_in = [mail.send(mine, mine, (gx, lax.rem(gy + d, 16))) for d in range(1, 16)]
    total = jnp.zeros((1, 768), F32)
    for c in range(CHUNKS):
        total = total + jnp.sum(wide(cot_all[c].reshape(256, 768)), axis=0, keepdims=True)
    grad_bias_down[...] = total
    total = jnp.zeros((1, 1536), F32)
    for c in range(CHUNKS):
        total = total + jnp.sum(wide(gh[c].reshape(256, 1536)), axis=0, keepdims=True)
    grad_bias_up[...] = total
    first_mean, second_mean = read_stats(stats_b, stats)
    scaled = gn[...] * gain[...]
    grad_patches[...] = (inv_std * (scaled - first_mean - standard[...] * second_mean)).astype(BF16)
    for copy in gain_in:
        copy.wait_recv()
    grad_gain[...] = jnp.sum(jnp.sum(gains[...], axis=0), axis=0, keepdims=True)
    mail.finish()
    store_wd.wait()
    store_wu.wait()


def shards(patches, norm_gain, w_up, bias_up, w_down, bias_down, cotangent):
    hbm, vmem = pl.BlockSpec(memory_space=pl.ANY), pl.BlockSpec(memory_space=pltpu.VMEM)
    shape = jax.ShapeDtypeStruct
    scratch = [
        pltpu.VMEM((64, 768), BF16),
        pltpu.VMEM((64, 768), F32),
        pltpu.VMEM((768, 1536), BF16),
        pltpu.VMEM((1536, 768), BF16),
        pltpu.VMEM((4, 2, 4, 2, 16, 768), BF16),
        pltpu.VMEM((4, 2, 4, 2, 16, 768), BF16),
        pltpu.VMEM((4, 4, 2, 32, 1536), BF16),
        pltpu.VMEM((4, 4, 32, 1536), BF16),
        pltpu.VMEM((4, 16, 1536), BF16),
        pltpu.VMEM((4, 16, 1536), BF16),
        pltpu.VMEM((4, 32, 1536), BF16),
        pltpu.VMEM((4, 32, 1536), BF16),
        pltpu.VMEM((4, 4, 2, 32, 1536), BF16),
        pltpu.VMEM((4, 32, 1536), BF16),
        pltpu.VMEM((4, 32, 1536), BF16),
        pltpu.VMEM((4, 2, 32, 1536), BF16),
        pltpu.VMEM((4, 2, 32, 1536), BF16),
        pltpu.VMEM((4, 32, 1536), BF16),
        pltpu.VMEM((4, 32, 1536), BF16),
        pltpu.VMEM((4, 4, 2, 32, 1536), BF16),
        pltpu.VMEM((4, 4, 2, 32, 1536), BF16),
    ]
    for _ in range(2):
        scratch += [
            pltpu.VMEM((4, 2, 4, 2, 16, 768), BF16),
            pltpu.VMEM((4, 2, 4, 16, 768), BF16),
            pltpu.VMEM((4, 4, 2, 16, 768), BF16),
            pltpu.VMEM((4, 16, 768), BF16),
            pltpu.VMEM((4, 16, 768), BF16),
        ]
    scratch += [
        pltpu.VMEM((64, 768), F32),
        pltpu.VMEM((8, 8, 128), F32),
        pltpu.VMEM((8, 8, 128), F32),
        pltpu.VMEM((16, 8, 768), F32),
        pltpu.VMEM((768, 1536), F32),
        pltpu.VMEM((1536, 768), F32),
        pltpu.SemaphoreType.DMA((9,)),
        pltpu.SemaphoreType.DMA((MESSAGES,)),
        pltpu.SemaphoreType.DMA((MESSAGES,)),
    ]
    outs = pl.pallas_call(
        kernel,
        out_shape=(
            shape((64, 768), BF16),
            shape((64, 768), BF16),
            shape((1, 768), F32),
            shape((768, 1536), F32),
            shape((1, 1536), F32),
            shape((1536, 768), F32),
            shape((1, 768), F32),
        ),
        in_specs=[hbm, vmem, hbm, vmem, hbm, vmem, hbm],
        out_specs=(vmem, vmem, vmem, hbm, vmem, hbm, vmem),
        scratch_shapes=scratch,
        compiler_params=pltpu.CompilerParams(
            collective_id=0, has_side_effects=True, vmem_limit_bytes=60 * 1024 * 1024
        ),
    )(
        patches, norm_gain.reshape(1, -1), w_up, bias_up.reshape(1, -1), w_down,
        bias_down.reshape(1, -1), cotangent,
    )
    mlp_out, grad_patches, grad_gain, grad_w_up, grad_bias_up, grad_w_down, grad_bias_down = outs
    return (
        mlp_out, grad_patches, grad_gain.reshape(-1), grad_w_up, grad_bias_up.reshape(-1),
        grad_w_down, grad_bias_down.reshape(-1),
    )


def solution(mesh):
    in_specs = (
        P("gy", "gx"),
        P("gx"),
        P("gx", "gy"),
        P("gy"),
        P("gy", "gx"),
        P("gx"),
        P("gy", "gx"),
    )
    out_specs = (
        P("gy", "gx"),
        P("gy", "gx"),
        P("gx"),
        P("gx", "gy"),
        P("gy"),
        P("gy", "gx"),
        P("gx"),
    )
    return jax.shard_map(shards, mesh=mesh, in_specs=in_specs, out_specs=out_specs, check_vma=False)
```

```python
import functools

import jax
import jax.numpy as jnp
from jax import lax
from jax.experimental import pallas as pl
from jax.experimental.pallas import tpu as pltpu
from jax.sharding import PartitionSpec as P

D = 6144
CHUNKS = 4
MESSAGES = 240

epsilon = 1e-06
inv_root_two = 0.7071067811865476
inv_root_two_pi = 0.3989422804014327

MESH = pl.DeviceIdType.MESH
F32 = jnp.float32
BF16 = jnp.bfloat16


def wide(value):
    return value.astype(F32)


def row(ref):
    return ref[...].reshape(1, ref.shape[0])


class Mail:
    def __init__(self, send_sems, recv_sems):
        self.send_sems, self.recv_sems, self.sent = send_sems, recv_sems, []

    def send(self, src, dst, device):
        at = len(self.sent)
        copy = pltpu.make_async_remote_copy(
            src_ref=src,
            dst_ref=dst,
            send_sem=self.send_sems.at[at],
            recv_sem=self.recv_sems.at[at],
            device_id=device,
            device_id_type=MESH,
        )
        copy.start()
        self.sent.append(copy)
        return copy

    def finish(self):
        for copy in self.sent:
            copy.wait_send()


def kernel(
    patches, gain, w_up, bias_up, w_down, bias_down, cotangent,
    mlp_out, grad_patches, grad_gain, grad_w_up, grad_bias_up, grad_w_down, grad_bias_down,
    own, standard, wu, wd, cot_all, nor_all,
    ga, ga_y, ga_m1r, ga_m1l, ga_l, ga_r,
    hid, hid_m1r, hid_m1l, hid_l, hid_r, hid_ys, hid_y,
    act, gh,
    mlp_g, mlp_sib, mlp_z, mlp_ys, mlp_y,
    gn_g, gn_sib, gn_z, gn_ys, gn_y, gn,
    stats_a, stats_b, gains, gwu, gwd,
    local_sems, send_sems, recv_sems,
):
    gx, gy = lax.axis_index("gx"), lax.axis_index("gy")
    x, y = lax.rem(gx, 4), lax.div(gx, 4)
    k, z, yh = lax.rem(gy, 2), lax.rem(lax.div(gy, 2), 4), lax.div(gy, 8)
    yo, ko, yho = 1 - y, 1 - k, 1 - yh
    xr, xo, xl = lax.rem(x + 1, 4), lax.rem(x + 2, 4), lax.rem(x + 3, 4)
    right, left, across = (y * 4 + xr, gy), (y * 4 + xl, gy), (yo * 4 + x, gy)
    sibling, far = (gx, yh * 8 + z * 2 + ko), (gx, yho * 8 + z * 2 + k)
    z_at = [lax.rem(z + d, 4) for d in range(4)]
    z_dev = [(gx, yh * 8 + z_at[d] * 2 + k) for d in range(4)]
    mail = Mail(send_sems, recv_sems)

    loads = [pltpu.make_async_copy(patches, own, local_sems.at[0])]
    for c in range(CHUNKS):
        loads.append(
            pltpu.make_async_copy(
                cotangent.at[pl.ds(16 * c, 16)], cot_all.at[c, yh, z, k], local_sems.at[1 + c]
            )
        )
    load_wd = pltpu.make_async_copy(w_down, wd, local_sems.at[5])
    load_wu = pltpu.make_async_copy(w_up, wu, local_sems.at[6])
    for copy in loads + [load_wd, load_wu]:
        copy.start()

    barrier = pltpu.get_barrier_semaphore()
    for d in range(1, 8):
        pl.semaphore_signal(barrier, inc=1, device_id=(lax.rem(gx + d, 8), gy), device_id_type=MESH)
    for d in range(1, 16):
        pl.semaphore_signal(barrier, inc=1, device_id=(gx, lax.rem(gy + d, 16)), device_id_type=MESH)
    pl.semaphore_wait(barrier, 22)

    far_in, z_in, sib_in = {}, {}, {}

    def to_far(name, full, c):
        piece = full.at[c, yh, z, k]
        far_in[name, c] = mail.send(piece, piece, far)

    def to_z(name, full, c):
        far_in[name, c].wait_recv()
        pair = full.at[c, :, z, k]
        z_in[name, c] = [mail.send(pair, pair, z_dev[d]) for d in (1, 2, 3)]

    def to_sibling(name, full, c):
        for copy in z_in[name, c]:
            copy.wait_recv()
        half = full.at[c, :, :, k]
        sib_in[name, c] = mail.send(half, half, sibling)

    def post_stats(box, first, second):
        lane = lax.broadcasted_iota(jnp.int32, (64, 128), 1)
        table = jnp.where(lane == 0, first, jnp.where(lane == 1, second, 0.0))
        table = jnp.concatenate([table, jnp.zeros((64, 128), F32)], axis=0)
        box[gx] = jnp.transpose(table)[:8]
        mine = box.at[gx]
        return [mail.send(mine, mine, (lax.rem(gx + d, 8), gy)) for d in range(1, 8)]

    def read_stats(box, copies):
        for copy in copies:
            copy.wait_recv()
        total = jnp.sum(box[...], axis=0)
        table = jnp.transpose(jnp.concatenate([total, jnp.zeros((120, 128), F32)], axis=0))
        return table[:64, 0:1] / D, table[:64, 1:2] / D

    for c in range(CHUNKS):
        loads[1 + c].wait()
        to_far("cot", cot_all, c)
    loads[0].wait()
    values = wide(own[...])
    stats = post_stats(
        stats_a,
        jnp.sum(values, axis=1, keepdims=True),
        jnp.sum(values * values, axis=1, keepdims=True),
    )

    def columns(total, step, body):
        @pl.loop(0, total // step)
        def _(n):
            body(pl.ds(pl.multiple_of(n * step, step), step))

    def multiply(left_value, right_ref, transposed, out, c, shape, total, step):
        def body(cols):
            if transposed:
                product = lax.dot_general(
                    left_value(), right_ref[cols, :], (((1,), (1,)), ((), ())),
                    preferred_element_type=F32,
                )
            else:
                product = jnp.dot(left_value(), right_ref[:, cols], preferred_element_type=F32)
            out[(c,) + (slice(None),) * (len(shape)) + (cols,)] = product.astype(BF16).reshape(
                shape + (step,)
            )

        columns(total, step, body)

    rows_gx, rows_gy = (4, 2, 32), (2, 4, 2, 16)

    def make_ga(c):
        sib_in["cot", c].wait_recv()
        if c == 0:
            load_wd.wait()
        multiply(lambda: cot_all[c].reshape(256, 768), wd, True, ga, c, rows_gx, 1536, 512)

    def make_hid(c):
        sib_in["nor", c].wait_recv()
        if c == 0:
            load_wu.wait()
        multiply(lambda: nor_all[c].reshape(256, 768), wu, False, hid, c, rows_gx, 1536, 512)

    def make_mlp(c):
        multiply(lambda: act[c].reshape(256, 1536), wd, False, mlp_g, c, rows_gy, 768, 256)

    def make_gn(c):
        multiply(lambda: gh[c].reshape(256, 1536), wu, True, gn_g, c, rows_gy, 768, 256)

    def weight_grad(out, left_ref, right_ref, c, rows, width):
        right_width = 768 + 1536 - rows

        def body(n):
            cols = pl.ds(pl.multiple_of(n * width, width), width)
            left_value = left_ref[(c,) + (slice(None),) * (len(left_ref.shape) - 2) + (cols,)]
            product = lax.dot_general(
                left_value.reshape(256, width), right_ref[c].reshape(256, right_width),
                (((0,), (0,)), ((), ())), preferred_element_type=F32,
            )
            if c == 0:
                out[cols, :] = product
            else:
                out[cols, :] += product

        pl.loop(0, rows // width)(body)

    ga_in, hid_in, act_in, gh_in = {}, {}, {}, {}
    top, low = pl.ds(0, 16), pl.ds(16, 16)

    def ga1(c):
        ga_in[c] = [mail.send(ga.at[c, :, yo], ga_y.at[c], across)]

    def ga2(c):
        ga_in[c][0].wait_recv()
        for t in (xo, xr, xl):
            ga[c, t, y] = (wide(ga[c, t, y]) + wide(ga_y[c, t])).astype(BF16)
        ga_in[c] = [
            mail.send(ga.at[c, xo, y, top], ga_m1r.at[c], right),
            mail.send(ga.at[c, xo, y, low], ga_m1l.at[c], left),
            mail.send(ga.at[c, xr, y, low], ga_l.at[c, low], right),
            mail.send(ga.at[c, xl, y, top], ga_r.at[c, top], left),
        ]

    def ga3(c):
        ga_in[c][0].wait_recv()
        ga[c, xr, y, top] = (wide(ga[c, xr, y, top]) + wide(ga_m1r[c])).astype(BF16)
        first = mail.send(ga.at[c, xr, y, top], ga_l.at[c, top], right)
        ga_in[c][1].wait_recv()
        ga[c, xl, y, low] = (wide(ga[c, xl, y, low]) + wide(ga_m1l[c])).astype(BF16)
        second = mail.send(ga.at[c, xl, y, low], ga_r.at[c, low], left)
        ga_in[c] = ga_in[c][2:] + [first, second]

    def ga4(c):
        for copy in ga_in[c]:
            copy.wait_recv()

    def hid1(c):
        hid_in[c] = [
            mail.send(hid.at[c, xo, 0], hid_m1r.at[c], right),
            mail.send(hid.at[c, xo, 1], hid_m1l.at[c], left),
            mail.send(hid.at[c, xr, 1], hid_l.at[c, 1], right),
            mail.send(hid.at[c, xl, 0], hid_r.at[c, 0], left),
        ]

    def hid2(c):
        hid_in[c][0].wait_recv()
        hid[c, xr, 0] = (wide(hid[c, xr, 0]) + wide(hid_m1r[c])).astype(BF16)
        first = mail.send(hid.at[c, xr, 0], hid_l.at[c, 0], right)
        hid_in[c][1].wait_recv()
        hid[c, xl, 1] = (wide(hid[c, xl, 1]) + wide(hid_m1l[c])).astype(BF16)
        second = mail.send(hid.at[c, xl, 1], hid_r.at[c, 1], left)
        hid_in[c] = hid_in[c][2:] + [first, second]

    def hid_sum(c, at):
        return wide(hid[c, x, at]) + wide(hid_l[c, at]) + wide(hid_r[c, at])

    def hid3(c):
        for copy in hid_in[c]:
            copy.wait_recv()
        hid_ys[c] = hid_sum(c, yo).astype(BF16)
        hid_in[c] = [mail.send(hid_ys.at[c], hid_y.at[c], across)]

    def hid4(c):
        hid_in[c][0].wait_recv()

    def activate(c):
        ga4(c)
        hid4(c)
        hidden = hid_sum(c, y) + wide(hid_y[c]) + row(bias_up)
        phi = 0.5 * (1.0 + lax.erf(hidden * inv_root_two))
        act[c, x, y] = (hidden * phi).astype(BF16)
        total = wide(ga[c, x, y]) + wide(ga_y[c, x]) + wide(ga_l[c]) + wide(ga_r[c])
        slope = phi + hidden * jnp.exp(-0.5 * hidden * hidden) * inv_root_two_pi
        gh[c, x, y] = (total * slope).astype(BF16)

    def act1(c):
        piece = act.at[c, x, y]
        act_in[c] = [mail.send(piece, piece, device) for device in (across, right, left)]

    def act2(c):
        act_in[c][0].wait_recv()
        piece = act.at[c, x, yo]
        act_in[c] = act_in[c][1:] + [mail.send(piece, piece, device) for device in (right, left)]

    def act3(c):
        for copy in act_in[c]:
            copy.wait_recv()
        act_in[c] = [
            mail.send(act.at[c, xl, 0], act.at[c, xl, 0], right),
            mail.send(act.at[c, xr, 1], act.at[c, xr, 1], left),
        ]

    def act4(c):
        for copy in act_in[c]:
            copy.wait_recv()

    def gh1(c):
        piece = gh.at[c, x, y]
        gh_in[c] = [mail.send(piece, piece, device) for device in (right, left, across)]

    def gh2(c):
        from_left, from_right, from_across = gh_in[c]
        from_left.wait_recv()
        first = mail.send(gh.at[c, xl, y, top], gh.at[c, xl, y, top], right)
        across_left = mail.send(gh.at[c, xl, y], gh.at[c, xl, y], across)
        from_right.wait_recv()
        second = mail.send(gh.at[c, xr, y, low], gh.at[c, xr, y, low], left)
        across_right = mail.send(gh.at[c, xr, y], gh.at[c, xr, y], across)
        gh_in[c] = [first, second, from_across, across_left, across_right]

    def gh3(c):
        gh_in[c][0].wait_recv()
        gh_in[c][1].wait_recv()
        gh_in[c] = gh_in[c][2:] + [mail.send(gh.at[c, xo, y], gh.at[c, xo, y], across)]

    def gh4(c):
        for copy in gh_in[c]:
            copy.wait_recv()

    boxes = {"mlp": (mlp_g, mlp_sib, mlp_z, mlp_ys, mlp_y), "gn": (gn_g, gn_sib, gn_z, gn_ys, gn_y)}
    back = {}

    def back0(name, c):
        part, sib, _, _, _ = boxes[name]
        back[name, c] = mail.send(part.at[c, :, :, ko], sib.at[c], sibling)

    def back1(name, c):
        part, sib, z_box, _, _ = boxes[name]
        back[name, c].wait_recv()
        part[c, :, :, k] = (wide(part[c, :, :, k]) + wide(sib[c])).astype(BF16)
        back[name, c] = [
            mail.send(part.at[c, :, z_at[d], k], z_box.at[c, z], z_dev[d]) for d in (1, 2, 3)
        ]

    def back_sum(name, c, at):
        part, _, z_box, _, _ = boxes[name]
        total = wide(part[c, at, z, k])
        for d in (1, 2, 3):
            total = total + wide(z_box[c, z_at[d], at])
        return total

    def back2(name, c):
        _, _, _, ys, y_box = boxes[name]
        for copy in back[name, c]:
            copy.wait_recv()
        ys[c] = back_sum(name, c, yho).astype(BF16)
        back[name, c] = mail.send(ys.at[c], y_box.at[c], far)

    def back3(name, c):
        back[name, c].wait_recv()
        total = back_sum(name, c, yh) + wide(boxes[name][4][c])
        if name == "mlp":
            mlp_out[pl.ds(16 * c, 16), :] = (total + row(bias_down)).astype(BF16)
        else:
            gn[pl.ds(16 * c, 16), :] = total

    for c in range(CHUNKS):
        to_z("cot", cot_all, c)
    row_mean, square_mean = read_stats(stats_a, stats)
    inv_std = lax.rsqrt(square_mean - row_mean * row_mean + epsilon)
    normal = (values - row_mean) * inv_std
    standard[...] = normal
    normed = (normal * row(gain)).astype(BF16)
    for c in range(CHUNKS):
        nor_all[c, yh, z, k] = normed[16 * c : 16 * c + 16]
        to_far("nor", nor_all, c)

    def cot3(c):
        to_sibling("cot", cot_all, c)

    def nor3(c):
        to_sibling("nor", nor_all, c)

    def start_ga(c):
        make_ga(c)
        ga1(c)

    def start_hid(c):
        make_hid(c)
        hid1(c)

    def start_act(c):
        activate(c)
        act1(c)
        gh1(c)

    def start_mlp(c):
        act4(c)
        make_mlp(c)
        back0("mlp", c)

    def start_gn(c):
        gh4(c)
        make_gn(c)
        back0("gn", c)

    def grad_down(c):
        weight_grad(gwd, act, cot_all, c, 1536, 256)

    def grad_up(c):
        weight_grad(gwu, nor_all, gh, c, 768, 256)

    cot3(0)
    start_ga(0)
    cot3(1)
    for c in range(CHUNKS):
        to_z("nor", nor_all, c)
    start_ga(1)
    cot3(2)
    nor3(0)
    ga2(0)
    start_hid(0)
    start_ga(2)
    cot3(3)
    nor3(1)
    ga3(0)
    ga2(1)
    hid2(0)
    start_hid(1)
    start_ga(3)
    nor3(2)
    ga3(1)
    ga2(2)
    hid3(0)
    hid2(1)
    start_hid(2)
    start_act(0)
    nor3(3)
    ga3(2)
    ga2(3)
    hid3(1)
    hid2(2)
    act2(0)
    start_hid(3)
    start_act(1)
    gh2(0)
    ga3(3)
    hid3(2)
    hid2(3)
    act3(0)
    act2(1)
    start_act(2)
    gh3(0)
    gh2(1)
    hid3(3)
    start_mlp(0)
    act3(1)
    act2(2)
    start_act(3)
    start_gn(0)
    grad_down(0)
    gh3(1)
    gh2(2)
    back1("mlp", 0)
    start_mlp(1)
    act3(2)
    act2(3)
    back1("gn", 0)
    grad_up(0)
    start_gn(1)
    gh3(2)
    gh2(3)
    back2("mlp", 0)
    back1("mlp", 1)
    grad_down(1)
    start_mlp(2)
    act3(3)
    back2("gn", 0)
    back1("gn", 1)
    start_gn(2)
    gh3(3)
    grad_up(1)
    back3("mlp", 0)
    back2("mlp", 1)
    back1("mlp", 2)
    start_mlp(3)
    grad_down(2)
    back3("gn", 0)
    back2("gn", 1)
    back1("gn", 2)
    grad_up(2)
    back3("mlp", 1)
    back2("mlp", 2)
    start_gn(3)
    back1("mlp", 3)
    grad_down(3)
    store_wd = pltpu.make_async_copy(gwd, grad_w_down, local_sems.at[7])
    store_wd.start()
    back3("gn", 1)
    back2("gn", 2)
    back1("gn", 3)
    back3("mlp", 2)
    back2("mlp", 3)
    back3("gn", 2)
    grad_up(3)
    store_wu = pltpu.make_async_copy(gwu, grad_w_up, local_sems.at[8])
    store_wu.start()
    back2("gn", 3)
    back3("mlp", 3)
    back3("gn", 3)

    grad_normed = gn[...]
    normal = standard[...]
    weighted = grad_normed * normal
    gains[gy] = jnp.sum(weighted.reshape(8, 8, 768), axis=0)
    scaled = grad_normed * row(gain)
    stats = post_stats(
        stats_b,
        jnp.sum(scaled, axis=1, keepdims=True),
        jnp.sum(scaled * normal, axis=1, keepdims=True),
    )
    mine = gains.at[gy]
    gain_in = [mail.send(mine, mine, (gx, lax.rem(gy + d, 16))) for d in range(1, 16)]
    total = jnp.zeros((1, 768), F32)
    for c in range(CHUNKS):
        total = total + jnp.sum(wide(cot_all[c].reshape(256, 768)), axis=0, keepdims=True)
    grad_bias_down[...] = total
    total = jnp.zeros((1, 1536), F32)
    for c in range(CHUNKS):
        total = total + jnp.sum(wide(gh[c].reshape(256, 1536)), axis=0, keepdims=True)
    grad_bias_up[...] = total
    first_mean, second_mean = read_stats(stats_b, stats)
    scaled = gn[...] * row(gain)
    grad_patches[...] = (inv_std * (scaled - first_mean - standard[...] * second_mean)).astype(BF16)
    for copy in gain_in:
        copy.wait_recv()
    grad_gain[...] = jnp.sum(jnp.sum(gains[...], axis=0), axis=0, keepdims=True)
    mail.finish()
    store_wd.wait()
    store_wu.wait()


PIECES = 4


def finish(
    mlp_in, patches_in, gain_in, w_up_in, bias_up_in, w_down_in, bias_down_in,
    mlp_out, grad_patches, grad_gain, grad_w_up, grad_bias_up, grad_w_down, grad_bias_down,
    up, down, in_sems, out_sems,
):
    moves = []
    for source, held, target in ((w_down_in, down, grad_w_down), (w_up_in, up, grad_w_up)):
        height = held.shape[0] // PIECES
        for p in range(PIECES):
            piece, at = pl.ds(p * height, height), len(moves)
            moves.append(
                (
                    pltpu.make_async_copy(source.at[piece], held.at[piece], in_sems.at[at]),
                    pltpu.make_async_copy(held.at[piece], target.at[piece], out_sems.at[at]),
                )
            )
    for load, _ in moves:
        load.start()
    mlp_out[...] = mlp_in[...]
    grad_patches[...] = patches_in[...]
    grad_gain[...] = gain_in[...].reshape(768)
    grad_bias_up[...] = bias_up_in[...].reshape(1536)
    grad_bias_down[...] = bias_down_in[...].reshape(768)
    for load, store in moves:
        load.wait()
        store.start()
    for _, store in moves:
        store.wait()


def shards(patches, norm_gain, w_up, bias_up, w_down, bias_down, cotangent):
    hbm, vmem = pl.BlockSpec(memory_space=pl.ANY), pl.BlockSpec(memory_space=pltpu.VMEM)
    shape = jax.ShapeDtypeStruct
    scratch = [
        pltpu.VMEM((64, 768), BF16),
        pltpu.VMEM((64, 768), F32),
        pltpu.VMEM((768, 1536), BF16),
        pltpu.VMEM((1536, 768), BF16),
        pltpu.VMEM((4, 2, 4, 2, 16, 768), BF16),
        pltpu.VMEM((4, 2, 4, 2, 16, 768), BF16),
        pltpu.VMEM((4, 4, 2, 32, 1536), BF16),
        pltpu.VMEM((4, 4, 32, 1536), BF16),
        pltpu.VMEM((4, 16, 1536), BF16),
        pltpu.VMEM((4, 16, 1536), BF16),
        pltpu.VMEM((4, 32, 1536), BF16),
        pltpu.VMEM((4, 32, 1536), BF16),
        pltpu.VMEM((4, 4, 2, 32, 1536), BF16),
        pltpu.VMEM((4, 32, 1536), BF16),
        pltpu.VMEM((4, 32, 1536), BF16),
        pltpu.VMEM((4, 2, 32, 1536), BF16),
        pltpu.VMEM((4, 2, 32, 1536), BF16),
        pltpu.VMEM((4, 32, 1536), BF16),
        pltpu.VMEM((4, 32, 1536), BF16),
        pltpu.VMEM((4, 4, 2, 32, 1536), BF16),
        pltpu.VMEM((4, 4, 2, 32, 1536), BF16),
    ]
    for _ in range(2):
        scratch += [
            pltpu.VMEM((4, 2, 4, 2, 16, 768), BF16),
            pltpu.VMEM((4, 2, 4, 16, 768), BF16),
            pltpu.VMEM((4, 4, 2, 16, 768), BF16),
            pltpu.VMEM((4, 16, 768), BF16),
            pltpu.VMEM((4, 16, 768), BF16),
        ]
    scratch += [
        pltpu.VMEM((64, 768), F32),
        pltpu.VMEM((8, 8, 128), F32),
        pltpu.VMEM((8, 8, 128), F32),
        pltpu.VMEM((16, 8, 768), F32),
        pltpu.VMEM((768, 1536), F32),
        pltpu.VMEM((1536, 768), F32),
        pltpu.SemaphoreType.DMA((9,)),
        pltpu.SemaphoreType.DMA((MESSAGES,)),
        pltpu.SemaphoreType.DMA((MESSAGES,)),
    ]
    outs = pl.pallas_call(
        kernel,
        out_shape=(
            shape((64, 768), BF16),
            shape((64, 768), BF16),
            shape((1, 768), F32),
            shape((768, 1536), F32),
            shape((1, 1536), F32),
            shape((1536, 768), F32),
            shape((1, 768), F32),
        ),
        in_specs=[hbm, vmem, hbm, vmem, hbm, vmem, hbm],
        out_specs=(vmem, vmem, vmem, hbm, vmem, hbm, vmem),
        scratch_shapes=scratch,
        compiler_params=pltpu.CompilerParams(
            collective_id=0, has_side_effects=True, vmem_limit_bytes=60 * 1024 * 1024
        ),
    )(
        patches, norm_gain, w_up, bias_up, w_down, bias_down, cotangent,
    )
    return pl.pallas_call(
        finish,
        out_shape=(
            shape((64, 768), BF16),
            shape((64, 768), BF16),
            shape((768,), F32),
            shape((768, 1536), F32),
            shape((1536,), F32),
            shape((1536, 768), F32),
            shape((768,), F32),
        ),
        in_specs=[vmem, vmem, vmem, hbm, vmem, hbm, vmem],
        out_specs=(vmem, vmem, vmem, hbm, vmem, hbm, vmem),
        scratch_shapes=[
            pltpu.VMEM((768, 1536), F32),
            pltpu.VMEM((1536, 768), F32),
            pltpu.SemaphoreType.DMA((2 * PIECES,)),
            pltpu.SemaphoreType.DMA((2 * PIECES,)),
        ],
        compiler_params=pltpu.CompilerParams(vmem_limit_bytes=67043328),
    )(*outs)


def solution(mesh):
    in_specs = (
        P("gy", "gx"),
        P("gx"),
        P("gx", "gy"),
        P("gy"),
        P("gy", "gx"),
        P("gx"),
        P("gy", "gx"),
    )
    out_specs = (
        P("gy", "gx"),
        P("gy", "gx"),
        P("gx"),
        P("gx", "gy"),
        P("gy"),
        P("gy", "gx"),
        P("gx"),
    )
    return jax.shard_map(shards, mesh=mesh, in_specs=in_specs, out_specs=out_specs, check_vma=False)
```

```python
import functools

import jax
import jax.numpy as jnp
from jax import lax
from jax.experimental import pallas as pl
from jax.experimental.pallas import tpu as pltpu
from jax.sharding import PartitionSpec as P

D = 6144
CHUNKS = 4
GA_X = (0,)
GH_Y = (3,)
MESSAGES = 240

epsilon = 1e-06
inv_root_two = 0.7071067811865476
inv_root_two_pi = 0.3989422804014327

MESH = pl.DeviceIdType.MESH
F32 = jnp.float32
BF16 = jnp.bfloat16


def wide(value):
    return value.astype(F32)


def row(ref):
    return ref[...].reshape(1, ref.shape[0])


class Mail:
    def __init__(self, send_sems, recv_sems):
        self.send_sems, self.recv_sems, self.sent = send_sems, recv_sems, []

    def send(self, src, dst, device):
        at = len(self.sent)
        copy = pltpu.make_async_remote_copy(
            src_ref=src,
            dst_ref=dst,
            send_sem=self.send_sems.at[at],
            recv_sem=self.recv_sems.at[at],
            device_id=device,
            device_id_type=MESH,
        )
        copy.start()
        self.sent.append(copy)
        return copy

    def finish(self):
        for copy in self.sent:
            copy.wait_send()


def kernel(
    patches, gain, w_up, bias_up, w_down, bias_down, cotangent,
    mlp_out, grad_patches, grad_gain, grad_w_up, grad_bias_up, grad_w_down, grad_bias_down,
    own, standard, wu, wd, cot_all, nor_all,
    ga, ga_y, ga_m1r, ga_m1l, ga_l, ga_r,
    gax_m1r, gax_m1l, gax_l, gax_r, gax_ys, gax_y,
    hid, hid_m1r, hid_m1l, hid_l, hid_r, hid_ys, hid_y,
    act, gh,
    mlp_g, mlp_sib, mlp_z, mlp_ys, mlp_y,
    gn_g, gn_sib, gn_z, gn_ys, gn_y, gn,
    stats_a, stats_b, gains, gwu, gwd,
    local_sems, send_sems, recv_sems,
):
    gx, gy = lax.axis_index("gx"), lax.axis_index("gy")
    x, y = lax.rem(gx, 4), lax.div(gx, 4)
    k, z, yh = lax.rem(gy, 2), lax.rem(lax.div(gy, 2), 4), lax.div(gy, 8)
    yo, ko, yho = 1 - y, 1 - k, 1 - yh
    xr, xo, xl = lax.rem(x + 1, 4), lax.rem(x + 2, 4), lax.rem(x + 3, 4)
    right, left, across = (y * 4 + xr, gy), (y * 4 + xl, gy), (yo * 4 + x, gy)
    sibling, far = (gx, yh * 8 + z * 2 + ko), (gx, yho * 8 + z * 2 + k)
    z_at = [lax.rem(z + d, 4) for d in range(4)]
    z_dev = [(gx, yh * 8 + z_at[d] * 2 + k) for d in range(4)]
    mail = Mail(send_sems, recv_sems)

    loads = [pltpu.make_async_copy(patches, own, local_sems.at[0])]
    for c in range(CHUNKS):
        loads.append(
            pltpu.make_async_copy(
                cotangent.at[pl.ds(16 * c, 16)], cot_all.at[c, yh, z, k], local_sems.at[1 + c]
            )
        )
    load_wd = pltpu.make_async_copy(w_down, wd, local_sems.at[5])
    load_wu = pltpu.make_async_copy(w_up, wu, local_sems.at[6])
    for copy in loads + [load_wd, load_wu]:
        copy.start()

    barrier = pltpu.get_barrier_semaphore()
    for d in range(1, 8):
        pl.semaphore_signal(barrier, inc=1, device_id=(lax.rem(gx + d, 8), gy), device_id_type=MESH)
    for d in range(1, 16):
        pl.semaphore_signal(barrier, inc=1, device_id=(gx, lax.rem(gy + d, 16)), device_id_type=MESH)
    pl.semaphore_wait(barrier, 22)

    far_in, z_in, sib_in = {}, {}, {}

    def to_far(name, full, c):
        piece = full.at[c, yh, z, k]
        far_in[name, c] = mail.send(piece, piece, far)

    def to_z(name, full, c):
        far_in[name, c].wait_recv()
        pair = full.at[c, :, z, k]
        z_in[name, c] = [mail.send(pair, pair, z_dev[d]) for d in (1, 2, 3)]

    def to_sibling(name, full, c):
        for copy in z_in[name, c]:
            copy.wait_recv()
        half = full.at[c, :, :, k]
        sib_in[name, c] = mail.send(half, half, sibling)

    def post_stats(box, first, second):
        lane = lax.broadcasted_iota(jnp.int32, (64, 128), 1)
        table = jnp.where(lane == 0, first, jnp.where(lane == 1, second, 0.0))
        table = jnp.concatenate([table, jnp.zeros((64, 128), F32)], axis=0)
        box[gx] = jnp.transpose(table)[:8]
        mine = box.at[gx]
        return [mail.send(mine, mine, (lax.rem(gx + d, 8), gy)) for d in range(1, 8)]

    def read_stats(box, copies):
        for copy in copies:
            copy.wait_recv()
        total = jnp.sum(box[...], axis=0)
        table = jnp.transpose(jnp.concatenate([total, jnp.zeros((120, 128), F32)], axis=0))
        return table[:64, 0:1] / D, table[:64, 1:2] / D

    for c in range(CHUNKS):
        loads[1 + c].wait()
        to_far("cot", cot_all, c)
    loads[0].wait()
    values = wide(own[...])
    stats = post_stats(
        stats_a,
        jnp.sum(values, axis=1, keepdims=True),
        jnp.sum(values * values, axis=1, keepdims=True),
    )

    def columns(total, step, body):
        @pl.loop(0, total // step)
        def _(n):
            body(pl.ds(pl.multiple_of(n * step, step), step))

    def multiply(left_value, right_ref, transposed, out, c, shape, total, step):
        def body(cols):
            if transposed:
                product = lax.dot_general(
                    left_value(), right_ref[cols, :], (((1,), (1,)), ((), ())),
                    preferred_element_type=F32,
                )
            else:
                product = jnp.dot(left_value(), right_ref[:, cols], preferred_element_type=F32)
            out[(c,) + (slice(None),) * (len(shape)) + (cols,)] = product.astype(BF16).reshape(
                shape + (step,)
            )

        columns(total, step, body)

    rows_gx, rows_gy = (4, 2, 32), (2, 4, 2, 16)

    def make_ga(c):
        sib_in["cot", c].wait_recv()
        if c == 0:
            load_wd.wait()
        multiply(lambda: cot_all[c].reshape(256, 768), wd, True, ga, c, rows_gx, 1536, 512)

    def make_hid(c):
        sib_in["nor", c].wait_recv()
        if c == 0:
            load_wu.wait()
        multiply(lambda: nor_all[c].reshape(256, 768), wu, False, hid, c, rows_gx, 1536, 512)

    def make_mlp(c):
        multiply(lambda: act[c].reshape(256, 1536), wd, False, mlp_g, c, rows_gy, 768, 256)

    def make_gn(c):
        multiply(lambda: gh[c].reshape(256, 1536), wu, True, gn_g, c, rows_gy, 768, 256)

    def weight_grad(out, left_ref, right_ref, c, rows, width):
        right_width = 768 + 1536 - rows

        def body(n):
            cols = pl.ds(pl.multiple_of(n * width, width), width)
            left_value = left_ref[(c,) + (slice(None),) * (len(left_ref.shape) - 2) + (cols,)]
            product = lax.dot_general(
                left_value.reshape(256, width), right_ref[c].reshape(256, right_width),
                (((0,), (0,)), ((), ())), preferred_element_type=F32,
            )
            if c == 0:
                out[cols, :] = product
            else:
                out[cols, :] += product

        pl.loop(0, rows // width)(body)

    ga_in, hid_in, act_in, gh_in = {}, {}, {}, {}
    top, low = pl.ds(0, 16), pl.ds(16, 16)

    def ga1(c):
        ga_in[c] = [mail.send(ga.at[c, :, yo], ga_y.at[c], across)]

    def ga2(c):
        ga_in[c][0].wait_recv()
        for t in (xo, xr, xl):
            ga[c, t, y] = (wide(ga[c, t, y]) + wide(ga_y[c, t])).astype(BF16)
        ga_in[c] = [
            mail.send(ga.at[c, xo, y, top], ga_m1r.at[c], right),
            mail.send(ga.at[c, xo, y, low], ga_m1l.at[c], left),
            mail.send(ga.at[c, xr, y, low], ga_l.at[c, low], right),
            mail.send(ga.at[c, xl, y, top], ga_r.at[c, top], left),
        ]

    def ga3(c):
        ga_in[c][0].wait_recv()
        ga[c, xr, y, top] = (wide(ga[c, xr, y, top]) + wide(ga_m1r[c])).astype(BF16)
        first = mail.send(ga.at[c, xr, y, top], ga_l.at[c, top], right)
        ga_in[c][1].wait_recv()
        ga[c, xl, y, low] = (wide(ga[c, xl, y, low]) + wide(ga_m1l[c])).astype(BF16)
        second = mail.send(ga.at[c, xl, y, low], ga_r.at[c, low], left)
        ga_in[c] = ga_in[c][2:] + [first, second]

    def ga4(c):
        for copy in ga_in[c]:
            copy.wait_recv()

    def x_sum(part, l, r, c, at):
        return wide(part[c, x, at]) + wide(l[c, at]) + wide(r[c, at])

    def x_first(part, m1r, m1l, l, r, ys, y_box, came):
        def one(c):
            came[c] = [
                mail.send(part.at[c, xo, 0], m1r.at[c], right),
                mail.send(part.at[c, xo, 1], m1l.at[c], left),
                mail.send(part.at[c, xr, 1], l.at[c, 1], right),
                mail.send(part.at[c, xl, 0], r.at[c, 0], left),
            ]

        def two(c):
            came[c][0].wait_recv()
            part[c, xr, 0] = (wide(part[c, xr, 0]) + wide(m1r[c])).astype(BF16)
            first = mail.send(part.at[c, xr, 0], l.at[c, 0], right)
            came[c][1].wait_recv()
            part[c, xl, 1] = (wide(part[c, xl, 1]) + wide(m1l[c])).astype(BF16)
            second = mail.send(part.at[c, xl, 1], r.at[c, 1], left)
            came[c] = came[c][2:] + [first, second]

        def three(c):
            for copy in came[c]:
                copy.wait_recv()
            ys[c] = x_sum(part, l, r, c, yo).astype(BF16)
            came[c] = [mail.send(ys.at[c], y_box.at[c], across)]

        def four(c):
            came[c][0].wait_recv()

        return one, two, three, four

    hid1, hid2, hid3, hid4 = x_first(
        hid, hid_m1r, hid_m1l, hid_l, hid_r, hid_ys, hid_y, hid_in
    )
    gax = x_first(ga, gax_m1r, gax_m1l, gax_l, gax_r, gax_ys, gax_y, ga_in)
    gay = (ga1, ga2, ga3, ga4)

    def ga_step(n, c):
        (gax if c in GA_X else gay)[n - 1](c)

    def activate(c):
        ga_step(4, c)
        hid4(c)
        hidden = x_sum(hid, hid_l, hid_r, c, y) + wide(hid_y[c]) + row(bias_up)
        phi = 0.5 * (1.0 + lax.erf(hidden * inv_root_two))
        act[c, x, y] = (hidden * phi).astype(BF16)
        if c in GA_X:
            total = x_sum(ga, gax_l, gax_r, c, y) + wide(gax_y[c])
        else:
            total = wide(ga[c, x, y]) + wide(ga_y[c, x]) + wide(ga_l[c]) + wide(ga_r[c])
        slope = phi + hidden * jnp.exp(-0.5 * hidden * hidden) * inv_root_two_pi
        gh[c, x, y] = (total * slope).astype(BF16)

    def y_gather(full, came):
        def one(c):
            piece = full.at[c, x, y]
            came[c] = [mail.send(piece, piece, device) for device in (across, right, left)]

        def two(c):
            came[c][0].wait_recv()
            piece = full.at[c, x, yo]
            came[c] = came[c][1:] + [mail.send(piece, piece, device) for device in (right, left)]

        def three(c):
            for copy in came[c]:
                copy.wait_recv()
            came[c] = [
                mail.send(full.at[c, xl, 0], full.at[c, xl, 0], right),
                mail.send(full.at[c, xr, 1], full.at[c, xr, 1], left),
            ]

        def four(c):
            for copy in came[c]:
                copy.wait_recv()

        return one, two, three, four

    act1, act2, act3, act4 = y_gather(act, act_in)

    def gh1(c):
        piece = gh.at[c, x, y]
        gh_in[c] = [mail.send(piece, piece, device) for device in (right, left, across)]

    def gh2(c):
        from_left, from_right, from_across = gh_in[c]
        from_left.wait_recv()
        first = mail.send(gh.at[c, xl, y, top], gh.at[c, xl, y, top], right)
        across_left = mail.send(gh.at[c, xl, y], gh.at[c, xl, y], across)
        from_right.wait_recv()
        second = mail.send(gh.at[c, xr, y, low], gh.at[c, xr, y, low], left)
        across_right = mail.send(gh.at[c, xr, y], gh.at[c, xr, y], across)
        gh_in[c] = [first, second, from_across, across_left, across_right]

    def gh3(c):
        gh_in[c][0].wait_recv()
        gh_in[c][1].wait_recv()
        gh_in[c] = gh_in[c][2:] + [mail.send(gh.at[c, xo, y], gh.at[c, xo, y], across)]

    def gh4(c):
        for copy in gh_in[c]:
            copy.wait_recv()

    ghy, ghx = y_gather(gh, gh_in), (gh1, gh2, gh3, gh4)

    def gh_step(n, c):
        (ghy if c in GH_Y else ghx)[n - 1](c)

    boxes = {"mlp": (mlp_g, mlp_sib, mlp_z, mlp_ys, mlp_y), "gn": (gn_g, gn_sib, gn_z, gn_ys, gn_y)}
    back = {}

    def back0(name, c):
        part, sib, _, _, _ = boxes[name]
        back[name, c] = mail.send(part.at[c, :, :, ko], sib.at[c], sibling)

    def back1(name, c):
        part, sib, z_box, _, _ = boxes[name]
        back[name, c].wait_recv()
        part[c, :, :, k] = (wide(part[c, :, :, k]) + wide(sib[c])).astype(BF16)
        back[name, c] = [
            mail.send(part.at[c, :, z_at[d], k], z_box.at[c, z], z_dev[d]) for d in (1, 2, 3)
        ]

    def back_sum(name, c, at):
        part, _, z_box, _, _ = boxes[name]
        total = wide(part[c, at, z, k])
        for d in (1, 2, 3):
            total = total + wide(z_box[c, z_at[d], at])
        return total

    def back2(name, c):
        _, _, _, ys, y_box = boxes[name]
        for copy in back[name, c]:
            copy.wait_recv()
        ys[c] = back_sum(name, c, yho).astype(BF16)
        back[name, c] = mail.send(ys.at[c], y_box.at[c], far)

    def back3(name, c):
        back[name, c].wait_recv()
        total = back_sum(name, c, yh) + wide(boxes[name][4][c])
        if name == "mlp":
            mlp_out[pl.ds(16 * c, 16), :] = (total + row(bias_down)).astype(BF16)
        else:
            gn[pl.ds(16 * c, 16), :] = total

    for c in range(CHUNKS):
        to_z("cot", cot_all, c)
    row_mean, square_mean = read_stats(stats_a, stats)
    inv_std = lax.rsqrt(square_mean - row_mean * row_mean + epsilon)
    normal = (values - row_mean) * inv_std
    standard[...] = normal
    normed = (normal * row(gain)).astype(BF16)
    for c in range(CHUNKS):
        nor_all[c, yh, z, k] = normed[16 * c : 16 * c + 16]
        to_far("nor", nor_all, c)

    def cot3(c):
        to_sibling("cot", cot_all, c)

    def nor3(c):
        to_sibling("nor", nor_all, c)

    def start_ga(c):
        make_ga(c)
        ga_step(1, c)

    def start_hid(c):
        make_hid(c)
        hid1(c)

    def start_act(c):
        activate(c)
        act1(c)
        gh_step(1, c)

    def start_mlp(c):
        act4(c)
        make_mlp(c)
        back0("mlp", c)

    def start_gn(c):
        gh_step(4, c)
        make_gn(c)
        back0("gn", c)

    def grad_down(c):
        weight_grad(gwd, act, cot_all, c, 1536, 256)

    def grad_up(c):
        weight_grad(gwu, nor_all, gh, c, 768, 256)

    cot3(0)
    start_ga(0)
    cot3(1)
    for c in range(CHUNKS):
        to_z("nor", nor_all, c)
    start_ga(1)
    cot3(2)
    nor3(0)
    ga_step(2, 0)
    start_hid(0)
    start_ga(2)
    cot3(3)
    nor3(1)
    ga_step(3, 0)
    ga_step(2, 1)
    hid2(0)
    start_hid(1)
    start_ga(3)
    nor3(2)
    ga_step(3, 1)
    ga_step(2, 2)
    hid3(0)
    hid2(1)
    start_hid(2)
    start_act(0)
    nor3(3)
    ga_step(3, 2)
    ga_step(2, 3)
    hid3(1)
    hid2(2)
    act2(0)
    start_hid(3)
    start_act(1)
    gh_step(2, 0)
    ga_step(3, 3)
    hid3(2)
    hid2(3)
    act3(0)
    act2(1)
    start_act(2)
    gh_step(3, 0)
    gh_step(2, 1)
    hid3(3)
    start_mlp(0)
    act3(1)
    act2(2)
    start_act(3)
    start_gn(0)
    grad_down(0)
    gh_step(3, 1)
    gh_step(2, 2)
    back1("mlp", 0)
    start_mlp(1)
    act3(2)
    act2(3)
    back1("gn", 0)
    grad_up(0)
    start_gn(1)
    gh_step(3, 2)
    gh_step(2, 3)
    back2("mlp", 0)
    back1("mlp", 1)
    grad_down(1)
    start_mlp(2)
    act3(3)
    back2("gn", 0)
    back1("gn", 1)
    start_gn(2)
    gh_step(3, 3)
    grad_up(1)
    back3("mlp", 0)
    back2("mlp", 1)
    back1("mlp", 2)
    start_mlp(3)
    grad_down(2)
    back3("gn", 0)
    back2("gn", 1)
    back1("gn", 2)
    grad_up(2)
    back3("mlp", 1)
    back2("mlp", 2)
    start_gn(3)
    back1("mlp", 3)
    grad_down(3)
    store_wd = pltpu.make_async_copy(gwd, grad_w_down, local_sems.at[7])
    store_wd.start()
    back3("gn", 1)
    back2("gn", 2)
    back1("gn", 3)
    back3("mlp", 2)
    back2("mlp", 3)
    back3("gn", 2)
    grad_up(3)
    store_wu = pltpu.make_async_copy(gwu, grad_w_up, local_sems.at[8])
    store_wu.start()
    back2("gn", 3)
    back3("mlp", 3)
    back3("gn", 3)

    grad_normed = gn[...]
    normal = standard[...]
    weighted = grad_normed * normal
    gains[gy] = jnp.sum(weighted.reshape(8, 8, 768), axis=0)
    scaled = grad_normed * row(gain)
    stats = post_stats(
        stats_b,
        jnp.sum(scaled, axis=1, keepdims=True),
        jnp.sum(scaled * normal, axis=1, keepdims=True),
    )
    mine = gains.at[gy]
    gain_in = [mail.send(mine, mine, (gx, lax.rem(gy + d, 16))) for d in range(1, 16)]
    total = jnp.zeros((1, 768), F32)
    for c in range(CHUNKS):
        total = total + jnp.sum(wide(cot_all[c].reshape(256, 768)), axis=0, keepdims=True)
    grad_bias_down[...] = total
    total = jnp.zeros((1, 1536), F32)
    for c in range(CHUNKS):
        total = total + jnp.sum(wide(gh[c].reshape(256, 1536)), axis=0, keepdims=True)
    grad_bias_up[...] = total
    first_mean, second_mean = read_stats(stats_b, stats)
    scaled = gn[...] * row(gain)
    grad_patches[...] = (inv_std * (scaled - first_mean - standard[...] * second_mean)).astype(BF16)
    for copy in gain_in:
        copy.wait_recv()
    grad_gain[...] = jnp.sum(jnp.sum(gains[...], axis=0), axis=0, keepdims=True)
    mail.finish()
    store_wd.wait()
    store_wu.wait()


PIECES = 4


def finish(
    mlp_in, patches_in, gain_in, w_up_in, bias_up_in, w_down_in, bias_down_in,
    mlp_out, grad_patches, grad_gain, grad_w_up, grad_bias_up, grad_w_down, grad_bias_down,
    up, down, in_sems, out_sems,
):
    moves = []
    for source, held, target in ((w_down_in, down, grad_w_down), (w_up_in, up, grad_w_up)):
        height = held.shape[0] // PIECES
        for p in range(PIECES):
            piece, at = pl.ds(p * height, height), len(moves)
            moves.append(
                (
                    pltpu.make_async_copy(source.at[piece], held.at[piece], in_sems.at[at]),
                    pltpu.make_async_copy(held.at[piece], target.at[piece], out_sems.at[at]),
                )
            )
    for load, _ in moves:
        load.start()
    mlp_out[...] = mlp_in[...]
    grad_patches[...] = patches_in[...]
    grad_gain[...] = gain_in[...].reshape(768)
    grad_bias_up[...] = bias_up_in[...].reshape(1536)
    grad_bias_down[...] = bias_down_in[...].reshape(768)
    for load, store in moves:
        load.wait()
        store.start()
    for _, store in moves:
        store.wait()


def shards(patches, norm_gain, w_up, bias_up, w_down, bias_down, cotangent):
    hbm, vmem = pl.BlockSpec(memory_space=pl.ANY), pl.BlockSpec(memory_space=pltpu.VMEM)
    shape = jax.ShapeDtypeStruct
    scratch = [
        pltpu.VMEM((64, 768), BF16),
        pltpu.VMEM((64, 768), F32),
        pltpu.VMEM((768, 1536), BF16),
        pltpu.VMEM((1536, 768), BF16),
        pltpu.VMEM((4, 2, 4, 2, 16, 768), BF16),
        pltpu.VMEM((4, 2, 4, 2, 16, 768), BF16),
        pltpu.VMEM((4, 4, 2, 32, 1536), BF16),
        pltpu.VMEM((4, 4, 32, 1536), BF16),
        pltpu.VMEM((4, 16, 1536), BF16),
        pltpu.VMEM((4, 16, 1536), BF16),
        pltpu.VMEM((4, 32, 1536), BF16),
        pltpu.VMEM((4, 32, 1536), BF16),
        pltpu.VMEM((4, 32, 1536), BF16),
        pltpu.VMEM((4, 32, 1536), BF16),
        pltpu.VMEM((4, 2, 32, 1536), BF16),
        pltpu.VMEM((4, 2, 32, 1536), BF16),
        pltpu.VMEM((4, 32, 1536), BF16),
        pltpu.VMEM((4, 32, 1536), BF16),
        pltpu.VMEM((4, 4, 2, 32, 1536), BF16),
        pltpu.VMEM((4, 32, 1536), BF16),
        pltpu.VMEM((4, 32, 1536), BF16),
        pltpu.VMEM((4, 2, 32, 1536), BF16),
        pltpu.VMEM((4, 2, 32, 1536), BF16),
        pltpu.VMEM((4, 32, 1536), BF16),
        pltpu.VMEM((4, 32, 1536), BF16),
        pltpu.VMEM((4, 4, 2, 32, 1536), BF16),
        pltpu.VMEM((4, 4, 2, 32, 1536), BF16),
    ]
    for _ in range(2):
        scratch += [
            pltpu.VMEM((4, 2, 4, 2, 16, 768), BF16),
            pltpu.VMEM((4, 2, 4, 16, 768), BF16),
            pltpu.VMEM((4, 4, 2, 16, 768), BF16),
            pltpu.VMEM((4, 16, 768), BF16),
            pltpu.VMEM((4, 16, 768), BF16),
        ]
    scratch += [
        pltpu.VMEM((64, 768), F32),
        pltpu.VMEM((8, 8, 128), F32),
        pltpu.VMEM((8, 8, 128), F32),
        pltpu.VMEM((16, 8, 768), F32),
        pltpu.VMEM((768, 1536), F32),
        pltpu.VMEM((1536, 768), F32),
        pltpu.SemaphoreType.DMA((9,)),
        pltpu.SemaphoreType.DMA((MESSAGES,)),
        pltpu.SemaphoreType.DMA((MESSAGES,)),
    ]
    outs = pl.pallas_call(
        kernel,
        out_shape=(
            shape((64, 768), BF16),
            shape((64, 768), BF16),
            shape((1, 768), F32),
            shape((768, 1536), F32),
            shape((1, 1536), F32),
            shape((1536, 768), F32),
            shape((1, 768), F32),
        ),
        in_specs=[hbm, vmem, hbm, vmem, hbm, vmem, hbm],
        out_specs=(vmem, vmem, vmem, hbm, vmem, hbm, vmem),
        scratch_shapes=scratch,
        compiler_params=pltpu.CompilerParams(
            collective_id=0, has_side_effects=True, vmem_limit_bytes=60 * 1024 * 1024
        ),
    )(
        patches, norm_gain, w_up, bias_up, w_down, bias_down, cotangent,
    )
    return pl.pallas_call(
        finish,
        out_shape=(
            shape((64, 768), BF16),
            shape((64, 768), BF16),
            shape((768,), F32),
            shape((768, 1536), F32),
            shape((1536,), F32),
            shape((1536, 768), F32),
            shape((768,), F32),
        ),
        in_specs=[vmem, vmem, vmem, hbm, vmem, hbm, vmem],
        out_specs=(vmem, vmem, vmem, hbm, vmem, hbm, vmem),
        scratch_shapes=[
            pltpu.VMEM((768, 1536), F32),
            pltpu.VMEM((1536, 768), F32),
            pltpu.SemaphoreType.DMA((2 * PIECES,)),
            pltpu.SemaphoreType.DMA((2 * PIECES,)),
        ],
        compiler_params=pltpu.CompilerParams(vmem_limit_bytes=67043328),
    )(*outs)


def solution(mesh):
    in_specs = (
        P("gy", "gx"),
        P("gx"),
        P("gx", "gy"),
        P("gy"),
        P("gy", "gx"),
        P("gx"),
        P("gy", "gx"),
    )
    out_specs = (
        P("gy", "gx"),
        P("gy", "gx"),
        P("gx"),
        P("gx", "gy"),
        P("gy"),
        P("gy", "gx"),
        P("gx"),
    )
    return jax.shard_map(shards, mesh=mesh, in_specs=in_specs, out_specs=out_specs, check_vma=False)
```
